256 devices in a mesh: gz: 32 (over y, z_lo, core), gx: 8 (over x, z_hi).
Axes of the slice: x: 4, y: 4, z: 8 (z_hi: 2, z_lo: 4; z = z_hi * 4 + z_lo), core: 2. Of those that a mesh axis runs over, the one named last changes fastest.
Arguments:
- ending_rightward_adjoint: float32 [2, 2048, 2048], P(None, 'gz', 'gx'), may hold values from -6 to 6
- ending_leftward_adjoint: float32 [2, 2048, 2048], P(None, 'gz', 'gx'), may hold values from -6 to 6
- ending_population_adjoint: float32 [2048, 2048], P('gz', 'gx'), may hold values from -6 to 6
- ending_holeburn_adjoint: float32 [2048, 2048], P('gz', 'gx'), may hold values from -6 to 6
- history_rightward: bfloat16 [4, 2, 2048, 2048], P(None, None, 'gz', 'gx'), may hold values from -4 to 4
- history_leftward: bfloat16 [4, 2, 2048, 2048], P(None, None, 'gz', 'gx'), may hold values from -4 to 4
- history_population: bfloat16 [4, 2048, 2048], P(None, 'gz', 'gx'), may hold values from 0.5 to 2
- history_holeburn: bfloat16 [4, 2048, 2048], P(None, 'gz', 'gx'), may hold values from -4 to 4
- segment_passive_attenuation: bfloat16 [2048, 2048], P('gz', 'gx'), may hold values from 0.049804688 to 0.59765625
Outputs:
- forward_adjoint: float32 [2, 2048, 2048], P(None, 'gz', 'gx')
- backward_adjoint: float32 [2, 2048, 2048], P(None, 'gz', 'gx')
- carrier_adjoint: float32 [2048, 2048], P('gz', 'gx')
- grating_adjoint: float32 [2048, 2048], P('gz', 'gx')
- current_gradient: float32 [2048], P('gx')
The draws below stay inside these ranges and needn't reach their ends.
All inputs are finite; a program needn't handle non-finite values.
Results may differ from the reference program's by a relative error of at most 0.0004.
Values may be sent and summed in bfloat16 or wider, within the bound.
A program may use at most 64 MiB of HBM per device.

```python
import math
import jax
import jax.numpy as jnp
from jax import lax

TRANSVERSE_NODES = 2048
ADJOINT_PASSES = 4
AXIAL_SEGMENTS = 2048
DIFF = 512


def level_of(key, shape, shards, least, high):
    level = 1.0
    for position, blocks in shards:
        draws = jax.random.uniform(jax.random.fold_in(jax.random.fold_in(key, 6), position), (blocks,), jnp.float32, least / len(shards), high / len(shards))
        level = level * jnp.repeat(jnp.exp(draws), shape[position] // blocks).reshape((-1,) + (1,) * (len(shape) - 1 - position))
    return level


def normal_values(own_key, extent, scale, reach, cuts=(), held_as=jnp.bfloat16):
    entries = scale * jax.random.normal(own_key, extent, jnp.float32)
    if cuts:
        entries = entries * level_of(own_key, extent, cuts, -0.22, 0.18)
    return jnp.clip(entries, -reach, reach).astype(held_as)


def setup_inputs(seed: int = 0) -> dict:
    streams_of = jax.random.split(jax.random.key(seed), 10)
    ending_rightward_adjoint = normal_values(streams_of[0], (2, AXIAL_SEGMENTS, TRANSVERSE_NODES), 1.0, 6.0, ((1, 32), (2, 8)), jnp.float32)
    ending_leftward_adjoint = normal_values(streams_of[1], (2, AXIAL_SEGMENTS, TRANSVERSE_NODES), 1.0, 6.0, ((1, 32), (2, 8)), jnp.float32)
    ending_population_adjoint = normal_values(streams_of[2], (AXIAL_SEGMENTS, TRANSVERSE_NODES), 1.0, 6.0, ((0, 32), (1, 8)), jnp.float32)
    ending_holeburn_adjoint = normal_values(streams_of[3], (AXIAL_SEGMENTS, TRANSVERSE_NODES), 1.0, 6.0, ((0, 32), (1, 8)), jnp.float32)
    history_rightward = normal_values(streams_of[4], (ADJOINT_PASSES, 2, AXIAL_SEGMENTS, TRANSVERSE_NODES), 0.7, 4.0, ((2, 32), (3, 8)))
    history_leftward = normal_values(streams_of[5], (ADJOINT_PASSES, 2, AXIAL_SEGMENTS, TRANSVERSE_NODES), 0.7, 4.0, ((2, 32), (3, 8)))
    history_population = jnp.clip(0.5 + 1.5 * jax.random.uniform(streams_of[6], (ADJOINT_PASSES, AXIAL_SEGMENTS, TRANSVERSE_NODES), jnp.float32) ** level_of(streams_of[6], (ADJOINT_PASSES, AXIAL_SEGMENTS, TRANSVERSE_NODES), ((1, 32), (2, 8)), -0.2, 0.2), 0.5, 2.0).astype(jnp.bfloat16)
    history_holeburn = normal_values(streams_of[7], (ADJOINT_PASSES, AXIAL_SEGMENTS, TRANSVERSE_NODES), 0.5, 4.0, ((1, 32), (2, 8)))
    segment_passive_attenuation = jnp.clip(jnp.exp(math.log(0.59765625) - 2.4849066 * jax.random.uniform(streams_of[8], (AXIAL_SEGMENTS, TRANSVERSE_NODES), jnp.float32) ** level_of(streams_of[8], (AXIAL_SEGMENTS, TRANSVERSE_NODES), ((0, 32), (1, 8)), -0.2, 0.2)), 0.049804688, 0.59765625).astype(jnp.bfloat16)
    return {"ending_rightward_adjoint": ending_rightward_adjoint, "ending_leftward_adjoint": ending_leftward_adjoint, "ending_population_adjoint": ending_population_adjoint, "ending_holeburn_adjoint": ending_holeburn_adjoint, "history_rightward": history_rightward, "history_leftward": history_leftward, "history_population": history_population, "history_holeburn": history_holeburn, "segment_passive_attenuation": segment_passive_attenuation}


FRONT_FACET = 0.3
REAR_FACET = 0.9
GAIN_SLOPE_RATE = 0.3
ALPHA_LINEWIDTH = 2.0
COUPLING = 0.5
CLOCK_DELTA = 0.3
DENSITY_LIFETIME = 2.0
GRATING_LIFE = 0.75
TRANSVERSE_DIFFUS = 0.2

def diffract(stacked):
    width = stacked.shape[-1]
    wavenum = jnp.arange(width, dtype=jnp.int32)
    signed = jnp.where(wavenum < width // 2, wavenum, wavenum - width)
    angle = (signed * signed).astype(jnp.float32) * (DIFF / (width / 2) ** 2)
    spectrum = jnp.fft.fft(stacked[0] + 1j * stacked[1], axis=-1)
    result = jnp.fft.ifft(spectrum * jnp.exp(1j * angle), axis=-1)
    return jnp.stack([jnp.real(result), jnp.imag(result)])

def multiplier_revision(rightward_multiplier, leftward_multiplier, population_multiplier, holeburn_multiplier, measured_rightward, measured_leftward, rightward_wave, leftward_wave, population_level, holeburn_magnitude, attenuation_factor, transverse_curvature):
    rightward_inphase, rightward_quadrature = (rightward_wave[0], rightward_wave[1])
    leftward_inphase, leftward_quadrature = (leftward_wave[0], leftward_wave[1])
    measured_rightward_inphase, measured_rightward_quadrature = (measured_rightward[0], measured_rightward[1])
    measured_leftward_inphase, measured_leftward_quadrature = (measured_leftward[0], measured_leftward[1])
    surplus_population = population_level - 1.0
    amplification_inphase = 1.0 + 0.5 * (GAIN_SLOPE_RATE * surplus_population - attenuation_factor)
    amplification_quadrature = 0.5 * GAIN_SLOPE_RATE * ALPHA_LINEWIDTH * surplus_population
    joined_waves = COUPLING * holeburn_magnitude
    population_derivative = 2.0 * CLOCK_DELTA * GAIN_SLOPE_RATE * surplus_population * population_multiplier
    holeburn_derivative = 2.0 * CLOCK_DELTA * holeburn_multiplier
    revised_rightward_inphase = amplification_inphase * measured_rightward_inphase - amplification_quadrature * measured_rightward_quadrature + joined_waves * measured_leftward_quadrature - population_derivative * rightward_inphase + holeburn_derivative * leftward_inphase
    revised_rightward_quadrature = amplification_inphase * measured_rightward_quadrature + amplification_quadrature * measured_rightward_inphase - joined_waves * measured_leftward_inphase - population_derivative * rightward_quadrature + holeburn_derivative * leftward_quadrature
    revised_leftward_inphase = amplification_inphase * measured_leftward_inphase - amplification_quadrature * measured_leftward_quadrature + joined_waves * measured_rightward_quadrature - population_derivative * leftward_inphase + holeburn_derivative * rightward_inphase
    revised_leftward_quadrature = amplification_inphase * measured_leftward_quadrature + amplification_quadrature * measured_leftward_inphase - joined_waves * measured_rightward_inphase - population_derivative * leftward_quadrature + holeburn_derivative * rightward_quadrature
    light_intensity = rightward_inphase * rightward_inphase + rightward_quadrature * rightward_quadrature + leftward_inphase * leftward_inphase + leftward_quadrature * leftward_quadrature
    amplification_share = measured_rightward_inphase * (rightward_inphase + ALPHA_LINEWIDTH * rightward_quadrature) + measured_rightward_quadrature * (rightward_quadrature - ALPHA_LINEWIDTH * rightward_inphase) + measured_leftward_inphase * (leftward_inphase + ALPHA_LINEWIDTH * leftward_quadrature) + measured_leftward_quadrature * (leftward_quadrature - ALPHA_LINEWIDTH * leftward_inphase)
    revised_population = population_multiplier * (1.0 - CLOCK_DELTA / DENSITY_LIFETIME - CLOCK_DELTA * GAIN_SLOPE_RATE * light_intensity) + TRANSVERSE_DIFFUS * transverse_curvature + 0.5 * GAIN_SLOPE_RATE * amplification_share
    fresh_holeburn = holeburn_multiplier * (1.0 - CLOCK_DELTA / GRATING_LIFE) + COUPLING * (measured_rightward_quadrature * leftward_inphase - measured_rightward_inphase * leftward_quadrature + measured_leftward_quadrature * rightward_inphase - measured_leftward_inphase * rightward_quadrature)
    return (jnp.stack([revised_rightward_inphase, revised_rightward_quadrature]), jnp.stack([revised_leftward_inphase, revised_leftward_quadrature]), revised_population, fresh_holeburn)

def reference(ending_rightward_adjoint, ending_leftward_adjoint, ending_population_adjoint, ending_holeburn_adjoint, history_rightward, history_leftward, history_population, history_holeburn, segment_passive_attenuation):
    rightward_multiplier, leftward_multiplier = (ending_rightward_adjoint, ending_leftward_adjoint)
    population_multiplier, holeburn_multiplier = (ending_population_adjoint, ending_holeburn_adjoint)
    attenuation_factor = segment_passive_attenuation.astype(jnp.float32)
    zpos = jnp.arange(AXIAL_SEGMENTS, dtype=jnp.int32).astype(jnp.float32)
    scaling_factor = 1.0 + 2.0 * zpos / (AXIAL_SEGMENTS - 1)
    shape_curve = jnp.zeros((TRANSVERSE_NODES,), jnp.float32)
    for moment_position in range(ADJOINT_PASSES - 1, -1, -1):
        shape_curve = shape_curve + lax.optimization_barrier(jnp.sum(scaling_factor[:, None] * population_multiplier, axis=0))
        lam_fwd = jnp.concatenate([rightward_multiplier[:, 1:, :], FRONT_FACET * leftward_multiplier[:, -1:, :]], axis=1)
        lam_bwd = jnp.concatenate([REAR_FACET * rightward_multiplier[:, :1, :], leftward_multiplier[:, :-1, :]], axis=1)
        measured_rightward = diffract(lam_fwd)
        measured_leftward = diffract(lam_bwd)
        bordered_array = jnp.pad(population_multiplier, ((0, 0), (1, 1)))
        transverse_curvature = bordered_array[:, 2:] + bordered_array[:, :-2] - 2.0 * population_multiplier
        rightward_multiplier, leftward_multiplier, population_multiplier, holeburn_multiplier = multiplier_revision(rightward_multiplier, leftward_multiplier, population_multiplier, holeburn_multiplier, measured_rightward, measured_leftward, history_rightward[moment_position].astype(jnp.float32), history_leftward[moment_position].astype(jnp.float32), history_population[moment_position].astype(jnp.float32), history_holeburn[moment_position].astype(jnp.float32), attenuation_factor, transverse_curvature)
    derivative_vector = CLOCK_DELTA * shape_curve / math.sqrt(AXIAL_SEGMENTS)
    return (rightward_multiplier, leftward_multiplier, population_multiplier, holeburn_multiplier, derivative_vector)
```

```python
import functools
import math

import jax
import jax.numpy as jnp
import numpy as np
from jax import lax
from jax.experimental import pallas as pl
from jax.experimental.pallas import tpu as pltpu
from jax.sharding import PartitionSpec as P

DIFF = 512
FRONT_FACET = 0.3
REAR_FACET = 0.9
GAIN_SLOPE_RATE = 0.3
ALPHA_LINEWIDTH = 2.0
COUPLING = 0.5
CLOCK_DELTA = 0.3
DENSITY_LIFETIME = 2.0
GRATING_LIFE = 0.75
TRANSVERSE_DIFFUS = 0.2

MESH = pl.DeviceIdType.MESH
F32 = jnp.float32
BF16 = jnp.bfloat16

NGX = 8
NGZ = 32
ROWS = 64
COLS = 256
OWN = 8
LANES = 128
RADIX = 16
WIDTH = 2048
POWER = 16.0
SPAN = 210.0
TINY = 1e-30


def tables():
    ka = np.arange(RADIX, dtype=np.float64)
    bb = np.arange(LANES, dtype=np.float64)
    twist = 2.0 * np.pi * ka[:, None] * bb[None, :] / WIDTH
    wavenum = np.arange(RADIX)[:, None] + RADIX * np.arange(LANES)[None, :]
    signed = np.where(wavenum < WIDTH // 2, wavenum, wavenum - WIDTH).astype(np.float64)
    phase = signed * signed * (DIFF / (WIDTH / 2) ** 2)
    small = np.stack(
        [np.cos(twist), np.sin(twist), np.cos(phase) / WIDTH, np.sin(phase) / WIDTH]
    ).astype(np.float32)
    angle = 2.0 * np.pi * ((bb[:, None] * bb[None, :]) % LANES) / LANES
    c, s = np.cos(angle), np.sin(angle)
    forward = np.block([[c, -s], [s, c]])
    inverse = np.block([[c, s], [-s, c]])
    mats = []
    for m in (forward, inverse):
        high = m.astype(np.float32).astype(jnp.bfloat16)
        low = (m - high.astype(np.float64)).astype(np.float32).astype(jnp.bfloat16)
        mats += [high, low]
    return np.stack(mats), small


def encode(v, inverse_scale):
    t = jnp.log2(1.0 + jnp.abs(v) * inverse_scale) * POWER
    return jnp.exp2(jnp.where(v < 0.0, -t, t))


def decode(y, scale):
    t = jnp.log2(y.astype(F32)) * (1.0 / POWER)
    u = (jnp.exp2(jnp.abs(t)) - 1.0) * scale
    return jnp.where(t < 0.0, -u, u)


def largest(block):
    return jnp.max(jnp.max(block, axis=0, keepdims=True), axis=1, keepdims=True)


def dft(values, sign):
    n = len(values)
    if n == 1:
        return values
    even = dft(values[0::2], sign)
    odd = dft(values[1::2], sign)
    low, high = [], []
    for k in range(n // 2):
        angle = 2.0 * math.pi * k / n
        c, s = math.cos(angle), sign * math.sin(angle)
        re, im = odd[k]
        if k == 0:
            tr, ti = re, im
        elif 4 * k == n:
            tr, ti = (-im, re) if s > 0 else (im, -re)
        elif 8 * k == n:
            h = c
            tr, ti = ((re - im) * h, (re + im) * h) if s > 0 else ((re + im) * h, (im - re) * h)
        elif 8 * k == 3 * n:
            h = -c
            tr, ti = ((-re - im) * h, (re - im) * h) if s > 0 else ((im - re) * h, (-re - im) * h)
        else:
            tr, ti = re * c - im * s, re * s + im * c
        er, ei = even[k]
        low.append((er + tr, ei + ti))
        high.append((er - tr, ei - ti))
    return low + high


def split(x):
    high = x.astype(BF16)
    return high, (x - high.astype(F32)).astype(BF16)


def product(xh, xl, w, which):
    high, low = w[2 * which], w[2 * which + 1]
    a = jnp.dot(xh[...], high, preferred_element_type=F32)
    a += jnp.dot(xl[...], high, preferred_element_type=F32)
    return a + jnp.dot(xh[...], low, preferred_element_type=F32)


def diffract(uv, out, w, tb, xh, xl):
    for field in range(2):
        points = [(uv[2 * field, a], uv[2 * field + 1, a]) for a in range(RADIX)]
        for k, (re, im) in enumerate(dft(points, -1.0)):
            c, s = tb[0, k : k + 1, :], tb[1, k : k + 1, :]
            row = pl.ds(16 * k + 8 * field, 8)
            h, l = split(re * c + im * s)
            xh[row, 0:LANES], xl[row, 0:LANES] = h, l
            h, l = split(im * c - re * s)
            xh[row, LANES:], xl[row, LANES:] = h, l
    spectrum = product(xh, xl, w, 0)
    for k in range(RADIX):
        row = slice(16 * k, 16 * k + 16)
        c, s = tb[2, k : k + 1, :], tb[3, k : k + 1, :]
        re, im = spectrum[row, :LANES], spectrum[row, LANES:]
        h, l = split(re * c - im * s)
        xh[row, 0:LANES], xl[row, 0:LANES] = h, l
        h, l = split(re * s + im * c)
        xh[row, LANES:], xl[row, LANES:] = h, l
    back = product(xh, xl, w, 1)
    for field in range(2):
        points = []
        for k in range(RADIX):
            row = slice(16 * k + 8 * field, 16 * k + 8 * field + 8)
            c, s = tb[0, k : k + 1, :], tb[1, k : k + 1, :]
            re, im = back[row, :LANES], back[row, LANES:]
            points.append((re * c - im * s, im * c + re * s))
        for a, (re, im) in enumerate(dft(points, 1.0)):
            out[2 * field, a] = re
            out[2 * field + 1, a] = im


def revised(v, wave, level, mirror, loss, c, m, lap):
    vfr, vfi, vbr, vbi = v
    fr, fi, br, bi = wave
    e = level - 1.0
    hr = 1.0 + 0.5 * (GAIN_SLOPE_RATE * e - loss)
    hi = 0.5 * GAIN_SLOPE_RATE * ALPHA_LINEWIDTH * e
    j = COUPLING * mirror
    pd = 2.0 * CLOCK_DELTA * GAIN_SLOPE_RATE * e * c
    hd = 2.0 * CLOCK_DELTA * m
    pr = hr * vfr - hi * vfi + j * vbi - pd * fr + hd * br
    pi = hr * vfi + hi * vfr - j * vbr - pd * fi + hd * bi
    qr = hr * vbr - hi * vbi + j * vfi - pd * br + hd * fr
    qi = hr * vbi + hi * vbr - j * vfr - pd * bi + hd * fi
    light = fr * fr + fi * fi + br * br + bi * bi
    share = (
        vfr * (fr + ALPHA_LINEWIDTH * fi)
        + vfi * (fi - ALPHA_LINEWIDTH * fr)
        + vbr * (br + ALPHA_LINEWIDTH * bi)
        + vbi * (bi - ALPHA_LINEWIDTH * br)
    )
    cn = (
        c * (1.0 - CLOCK_DELTA / DENSITY_LIFETIME - CLOCK_DELTA * GAIN_SLOPE_RATE * light)
        + TRANSVERSE_DIFFUS * lap
        + 0.5 * GAIN_SLOPE_RATE * share
    )
    mn = m * (1.0 - CLOCK_DELTA / GRATING_LIFE) + COUPLING * (
        vfi * br - vfr * bi + vbi * fr - vbr * fi
    )
    return pr, pi, qr, qi, cn, mn


def place_of(g, b):
    x, zh, core = lax.div(b, 2), lax.rem(b, 2), lax.rem(g, 2)
    pos = x + zh * (7 - 2 * x)
    return pos + core * (7 - 2 * pos)


def owner_of(g, j):
    core = lax.rem(g, 2)
    pos = j + core * (7 - 2 * j)
    far = lax.div(pos, 4)
    return 2 * pos * (1 - far) + (2 * (7 - pos) + 1) * far


def rows_at(j):
    return pl.ds(pl.multiple_of(j * OWN, OWN), OWN)


def iota(axis):
    return lax.broadcasted_iota(jnp.int32, (OWN, LANES), axis)


def exchange_kernel(
    p_h, q_h, c_h, m_h, f_h, b_h, n_h, g_h, l_h, w_h, t_h,
    oc, oe, os,
    pq, w, tb, ch, co, ax, rc, ra, rh, rl, st, uv, vv, xh, xl,
    hs, hr, sacc, sb, sr, s2b, s2, s3b, s3, vo, eo,
    ls, ss, rs, cs, cr, hss, hrs, ys, yr, zs, zr,
):
    g, b = lax.axis_index("gz"), lax.axis_index("gx")
    me = place_of(g, b)
    y, r = lax.div(g, 8), lax.rem(g, 8)
    started = []

    loads = [
        (p_h, pq.at[0:2]),
        (q_h, pq.at[2:4]),
        (c_h, pq.at[4]),
        (m_h, pq.at[5]),
        (w_h, w),
        (t_h, tb),
    ]
    loads = [pltpu.make_async_copy(a, d, ls.at[i]) for i, (a, d) in enumerate(loads)]
    for load in loads:
        load.start()

    g_up, g_down = lax.rem(g + 1, NGZ), lax.rem(g + NGZ - 1, NGZ)
    chain = g * NGX + me
    after = lax.rem(chain + 1, NGZ * NGX)
    before = lax.rem(chain + NGZ * NGX - 1, NGZ * NGX)

    def row_device(q):
        qg = lax.div(q, NGX)
        return qg, owner_of(qg, lax.rem(q, NGX))

    dev_after, dev_before = row_device(after), row_device(before)
    y_peers = [(lax.rem(y + k, 4) * 8 + r, b) for k in range(1, 4)]
    z_peers = [(y * 8 + lax.rem(r + k, 8), b) for k in range(1, 8)]
    x_peers = [(g, lax.rem(b + k, NGX)) for k in range(1, NGX)]
    greet = x_peers + y_peers + z_peers + [(g_up, b), (g_down, b), dev_after, dev_before]
    barrier = pltpu.get_barrier_semaphore()
    for peer in greet:
        pl.semaphore_signal(barrier, inc=1, device_id=peer, device_id_type=MESH)

    for load in loads[:4]:
        load.wait()
    top_c = largest(jnp.max(jnp.abs(pq[4]).reshape(8, 8, COLS), axis=0))
    top_m = largest(jnp.max(jnp.abs(pq[5]).reshape(8, 8, COLS), axis=0))
    top_u = jnp.max(jnp.abs(pq[0:4]).reshape(32, 8, COLS), axis=0)
    sc_c = jnp.maximum(top_c, TINY) * (1.0 / SPAN)
    sc_m = jnp.maximum(top_m, TINY) * (1.0 / SPAN)
    for i, sc in ((4, sc_c), (5, sc_m)):
        inv = 1.0 / sc
        for t in range(8):
            rows = slice(8 * t, 8 * t + 8)
            co[i, rows] = encode(pq[i, rows], inv).astype(BF16)

    pl.semaphore_wait(barrier, len(greet))

    def remote(src, dst, send, recv, device):
        copy = pltpu.make_async_remote_copy(
            src_ref=src, dst_ref=dst, send_sem=send, recv_sem=recv,
            device_id=device, device_id_type=MESH,
        )
        copy.start()
        started.append(copy)
        return copy

    edge = [
        remote(p_h.at[:, 0:8, :], ch.at[0], cs.at[0], cr.at[0], (g_down, b)),
        remote(q_h.at[:, 56:64, :], ch.at[1], cs.at[1], cr.at[1], (g_up, b)),
    ]

    def spread(ident, src_of, dst):
        got = []
        for k in range(1, NGX):
            peer = lax.rem(b + k, NGX)
            src = src_of(peer, place_of(g, peer))
            got.append(remote(src, dst, ss.at[ident, k], rs.at[ident, k], (g, peer)))
        own = pltpu.make_async_copy(src_of(b, me), dst, rs.at[ident, 0])
        own.start()
        return got, own

    def arrive(group):
        for copies, own in group:
            for copy in copies:
                copy.wait_recv()
            own.wait()

    def history(step):
        base = 3 + 4 * (3 - step) + (1 if step < 3 else 0)
        slot = rh.at[3 - step]
        return [
            spread(base, lambda _, j: f_h.at[step, :, rows_at(j), :], slot.at[0:2, b]),
            spread(base + 1, lambda _, j: b_h.at[step, :, rows_at(j), :], slot.at[2:4, b]),
            spread(base + 2, lambda _, j: n_h.at[step, rows_at(j), :], slot.at[4, b]),
            spread(base + 3, lambda _, j: g_h.at[step, rows_at(j), :], slot.at[5, b]),
        ]

    got_hist = {3: history(3)}
    got_loss = [spread(7, lambda _, j: l_h.at[rows_at(j), :], rl.at[b])]
    got_cm = [spread(0, lambda _, j: co.at[4:6, rows_at(j), :], rc.at[4:6, b])]

    for copy in edge:
        copy.wait_recv()
    halo = jnp.maximum(jnp.max(jnp.abs(ch[0]), axis=0), jnp.max(jnp.abs(ch[1]), axis=0))
    first_block, last_block = g == 0, g == NGZ - 1
    use_halo_top = jnp.where(first_block & last_block, 0.0, 1.0)
    top_u = largest(jnp.maximum(top_u, halo * use_halo_top))
    sc_u = jnp.maximum(top_u, TINY) * (1.0 / SPAN)
    inv = 1.0 / sc_u
    wide_row = lax.broadcasted_iota(jnp.int32, (OWN, COLS), 0)
    for part in range(2):
        for t in range(8):
            rows = slice(8 * t, 8 * t + 8)
            block = pltpu.roll(pq[part, rows], 7, 0)
            if t < 7:
                edge_row = pq[part, 8 * t + 8 : 8 * t + 9]
            else:
                edge_row = jnp.where(
                    last_block, FRONT_FACET * pq[2 + part, 63:64], ch[0, part, 0:1]
                )
            block = jnp.where(wide_row == 7, edge_row, block)
            co[part, rows] = encode(block, inv).astype(BF16)
            block = pltpu.roll(pq[2 + part, rows], 1, 0)
            if t > 0:
                edge_row = pq[2 + part, 8 * t - 1 : 8 * t]
            else:
                edge_row = jnp.where(first_block, REAR_FACET * pq[part, 0:1], ch[1, part, 7:8])
            block = jnp.where(wide_row == 0, edge_row, block)
            co[2 + part, rows] = encode(block, inv).astype(BF16)
    row, lane = iota(0), iota(1)
    ax[...] = jnp.where(row == 0, sc_u, jnp.where(row == 1, sc_c, sc_m))
    got_ax = [spread(2, lambda _, j: ax, ra.at[b])]
    got_uv = [spread(1, lambda _, j: co.at[0:4, rows_at(j), :], rc.at[0:4, b])]
    got_hist[2] = history(2)

    for load in loads[4:]:
        load.wait()
    arrive(got_ax)
    arrive(got_uv)
    for a in range(RADIX):
        src, half = a // 2, pl.ds(LANES * (a % 2), LANES)
        scale = ra[src, 0:1, :]
        for i in range(4):
            uv[i, a] = decode(rc[i, src, :, half], scale)
    got_hist[1] = history(1)
    diffract(uv, vv, w, tb, xh, xl)

    arrive(got_cm)
    arrive(got_loss)
    for a in range(RADIX):
        src, half = a // 2, pl.ds(LANES * (a % 2), LANES)
        for i in (4, 5):
            st[i, a] = decode(rc[i, src, :, half], ra[src, i - 3 : i - 2, :])
    weight = 1.0 + (2.0 / (ROWS * NGZ - 1)) * (row + chain * OWN).astype(F32)
    for a in range(RADIX):
        sacc[a] = weight * st[4, a]

    first_rows, last_rows = chain == 0, chain == NGZ * NGX - 1

    def lateral(a):
        c = st[4, a]
        left, right = pltpu.roll(c, 1, 1), pltpu.roll(c, LANES - 1, 1)
        left_in = pltpu.roll(st[4, a - 1], 1, 1) if a > 0 else jnp.zeros_like(c)
        right_in = (
            pltpu.roll(st[4, a + 1], LANES - 1, 1) if a < RADIX - 1 else jnp.zeros_like(c)
        )
        left = jnp.where(lane == 0, left_in, left)
        right = jnp.where(lane == LANES - 1, right_in, right)
        return c, left, right

    halos = None
    for step in (3, 2, 1):
        slot = 3 - step
        arrive(got_hist[step])
        laps = []
        for a in range(RADIX):
            c, left, right = lateral(a)
            uv[0, a] = right - 2.0 * c + left
        for a in range(RADIX):
            src, half = a // 2, pl.ds(LANES * (a % 2), LANES)
            past = [rh[slot, i, src, :, half].astype(F32) for i in range(6)]
            new = revised(
                [vv[i, a] for i in range(4)], past[:4], past[4], past[5],
                rl[src, :, half].astype(F32), st[4, a], st[5, a], uv[0, a],
            )
            for i in range(6):
                st[i, a] = new[i]
            sacc[a] += weight * new[4]
            for i in range(2):
                hs[slot, 0, i, :, pl.ds(LANES * a, LANES)] = new[i][0:1]
                hs[slot, 1, i, :, pl.ds(LANES * a, LANES)] = new[2 + i][7:8]
        halos = [
            remote(hs.at[slot, 0], hr.at[slot, 0], hss.at[slot, 0], hrs.at[slot, 0], dev_before),
            remote(hs.at[slot, 1], hr.at[slot, 1], hss.at[slot, 1], hrs.at[slot, 1], dev_after),
        ]
        if step == 1:
            for a in range(RADIX):
                half = pl.ds(LANES * (a % 2), LANES)
                sb[a // 2, :, half] = jnp.sum(sacc[a], axis=0, keepdims=True)
            got_s = [spread(19, lambda peer, j: sb.at[peer], sr.at[b])]
            scales = []
            for i in (4, 5):
                top = jnp.abs(st[i, 0])
                for a in range(1, RADIX):
                    top = jnp.maximum(top, jnp.abs(st[i, a]))
                sc = jnp.maximum(largest(top), TINY) * (1.0 / SPAN)
                scales.append(sc)
                inv = 1.0 / sc
                for a in range(RADIX):
                    half = pl.ds(LANES * (a % 2), LANES)
                    vo[i, a // 2, :, half] = encode(st[i, a], inv).astype(BF16)
            got_out = [spread(16, lambda peer, j: vo.at[4:6, peer], oc.at[4:6, me])]
        for copy in halos:
            copy.wait_recv()
        energy = [jnp.zeros((OWN, LANES), F32), jnp.zeros((OWN, LANES), F32)]
        for a in range(RADIX):
            cols = pl.ds(LANES * a, LANES)
            for i in range(2):
                edge_row = jnp.where(
                    last_rows, FRONT_FACET * st[2 + i, a, 7:8], hr[slot, 0, i, :, cols]
                )
                u = jnp.where(row == 7, edge_row, pltpu.roll(st[i, a], 7, 0))
                edge_row = jnp.where(
                    first_rows, REAR_FACET * st[i, a, 0:1], hr[slot, 1, i, :, cols]
                )
                q = jnp.where(row == 0, edge_row, pltpu.roll(st[2 + i, a], 1, 0))
                uv[i, a] = u
                uv[2 + i, a] = q
                if step == 1:
                    energy = [energy[0] + u * u, energy[1] + q * q]
        if step == 1:
            norms = [jnp.sum(e, axis=1, keepdims=True) for e in energy]
            norm = jnp.sqrt(jnp.max(jnp.maximum(norms[0], norms[1]), axis=0, keepdims=True))
            sc_v = jnp.maximum(norm, TINY) * (1.0 / SPAN)
            marks = jnp.where(row == 0, sc_v, jnp.where(row == 1, scales[0], scales[1]))
            for block in range(NGX):
                _, left, _ = lateral(2 * block)
                _, _, right = lateral(2 * block + 1)
                tile = jnp.where(lane == 0, left, marks)
                eo[block] = jnp.where(lane == LANES - 1, right, tile)
            got_out.append(spread(17, lambda peer, j: eo.at[peer], oe.at[me]))
            arrive(got_s)
            total = sr[0]
            for k in range(1, NGX):
                total = total + sr[k]
            s2b[...] = total
            s2[0] = total
            got_y = [
                remote(s2b, s2.at[k], ys.at[k], yr.at[k], peer)
                for k, peer in enumerate(y_peers, 1)
            ]
        diffract(uv, vv, w, tb, xh, xl)

    for copy in got_y:
        copy.wait_recv()
    total = (s2[0] + s2[1]) + (s2[2] + s2[3])
    s3b[...] = total
    s3[0] = total
    got_z = [
        remote(s3b, s3.at[k], zs.at[k], zr.at[k], peer) for k, peer in enumerate(z_peers, 1)
    ]
    inv = 1.0 / sc_v
    for a in range(RADIX):
        half = pl.ds(LANES * (a % 2), LANES)
        for i in range(4):
            vo[i, a // 2, :, half] = encode(vv[i, a], inv).astype(BF16)
    got_out.append(spread(18, lambda peer, j: vo.at[0:4, peer], oc.at[0:4, me]))
    for copy in got_z:
        copy.wait_recv()
    total = s3[0]
    for k in range(1, NGX):
        total = total + s3[k]
    os[...] = total * (CLOCK_DELTA / math.sqrt(ROWS * NGZ))
    arrive(got_out)
    for copy in started:
        copy.wait_send()


def final_kernel(oc, oe, os, f, bw, n, g, l, po, qo, co, mo, so, edge):
    so[...] = os[...]
    lane = lax.broadcasted_iota(jnp.int32, (OWN, COLS), 1)
    for t in range(oc.shape[1]):
        rows = pl.ds(OWN * t, OWN)
        marks = oe[t]
        scale = [marks[i : i + 1, 64:65] for i in range(3)]
        v = [decode(oc[i, t], scale[0]) for i in range(4)]
        c = decode(oc[4, t], scale[1])
        m = decode(oc[5, t], scale[2])
        left = jnp.where(lane == 0, marks[:, 0:1], pltpu.roll(c, 1, 1))
        right = jnp.where(lane == COLS - 1, marks[:, 127:128], pltpu.roll(c, COLS - 1, 1))
        wave = [x[0, i, rows].astype(F32) for x in (f, bw) for i in range(2)]
        new = revised(
            v, wave, n[0, rows].astype(F32), g[0, rows].astype(F32), l[rows].astype(F32),
            c, m, right - 2.0 * c + left,
        )
        po[0, rows], po[1, rows] = new[0], new[1]
        qo[0, rows], qo[1, rows] = new[2], new[3]
        co[rows] = new[4]
        mo[rows] = new[5]


def per_device(p, q, c, m, f, bw, n, g, l):
    mats, small = tables()
    any_space = pl.BlockSpec(memory_space=pl.ANY)
    dma = pltpu.SemaphoreType.DMA
    codes, edges, sums = pl.pallas_call(
        exchange_kernel,
        out_shape=(
            jax.ShapeDtypeStruct((6, NGX, OWN, COLS), BF16),
            jax.ShapeDtypeStruct((NGX, OWN, LANES), F32),
            jax.ShapeDtypeStruct((1, COLS), F32),
        ),
        in_specs=[any_space] * 11,
        out_specs=(any_space, any_space, pl.BlockSpec(memory_space=pltpu.VMEM)),
        scratch_shapes=[
            pltpu.VMEM((6, ROWS, COLS), F32),
            pltpu.VMEM((4, COLS, COLS), BF16),
            pltpu.VMEM((4, RADIX, LANES), F32),
            pltpu.VMEM((2, 2, OWN, COLS), F32),
            pltpu.VMEM((6, ROWS, COLS), BF16),
            pltpu.VMEM((OWN, LANES), F32),
            pltpu.VMEM((6, NGX, OWN, COLS), BF16),
            pltpu.VMEM((NGX, OWN, LANES), F32),
            pltpu.VMEM((3, 6, NGX, OWN, COLS), BF16),
            pltpu.VMEM((NGX, OWN, COLS), BF16),
            pltpu.VMEM((6, RADIX, OWN, LANES), F32),
            pltpu.VMEM((4, RADIX, OWN, LANES), F32),
            pltpu.VMEM((4, RADIX, OWN, LANES), F32),
            pltpu.VMEM((COLS, COLS), BF16),
            pltpu.VMEM((COLS, COLS), BF16),
            pltpu.VMEM((3, 2, 2, 1, WIDTH), F32),
            pltpu.VMEM((3, 2, 2, 1, WIDTH), F32),
            pltpu.VMEM((RADIX, OWN, LANES), F32),
            pltpu.VMEM((NGX, 1, COLS), F32),
            pltpu.VMEM((NGX, 1, COLS), F32),
            pltpu.VMEM((1, COLS), F32),
            pltpu.VMEM((4, 1, COLS), F32),
            pltpu.VMEM((1, COLS), F32),
            pltpu.VMEM((8, 1, COLS), F32),
            pltpu.VMEM((6, NGX, OWN, COLS), BF16),
            pltpu.VMEM((NGX, OWN, LANES), F32),
            dma((6,)),
            dma((20, NGX)),
            dma((20, NGX)),
            dma((2,)),
            dma((2,)),
            dma((3, 2)),
            dma((3, 2)),
            dma((4,)),
            dma((4,)),
            dma((8,)),
            dma((8,)),
        ],
        compiler_params=pltpu.CompilerParams(collective_id=0, has_side_effects=True),
        name="exchange",
    )(p, q, c, m, f, bw, n, g, l, jnp.asarray(mats), jnp.asarray(small))

    parts = 4
    per, rows = NGX // parts, ROWS // parts
    pair = pl.BlockSpec((2, rows, COLS), lambda i: (0, i, 0))
    single = pl.BlockSpec((rows, COLS), lambda i: (i, 0))
    line = pl.BlockSpec((1, COLS), lambda i: (0, 0))
    po, qo, co, mo, so = pl.pallas_call(
        functools.partial(final_kernel, edge=None),
        grid=(parts,),
        out_shape=(
            jax.ShapeDtypeStruct(p.shape, F32),
            jax.ShapeDtypeStruct(q.shape, F32),
            jax.ShapeDtypeStruct(c.shape, F32),
            jax.ShapeDtypeStruct(m.shape, F32),
            jax.ShapeDtypeStruct((1, COLS), F32),
        ),
        in_specs=[
            pl.BlockSpec((6, per, OWN, COLS), lambda i: (0, i, 0, 0)),
            pl.BlockSpec((per, OWN, LANES), lambda i: (i, 0, 0)),
            line,
            pl.BlockSpec((1, 2, rows, COLS), lambda i: (0, 0, i, 0)),
            pl.BlockSpec((1, 2, rows, COLS), lambda i: (0, 0, i, 0)),
            pl.BlockSpec((1, rows, COLS), lambda i: (0, i, 0)),
            pl.BlockSpec((1, rows, COLS), lambda i: (0, i, 0)),
            single,
        ],
        out_specs=(pair, pair, single, single, line),
        name="last_step",
    )(codes, edges, sums, f, bw, n, g, l)
    return po, qo, co, mo, so.reshape(COLS)


def solution(mesh):
    in_specs = (
        P(None, "gz", "gx"),
        P(None, "gz", "gx"),
        P("gz", "gx"),
        P("gz", "gx"),
        P(None, None, "gz", "gx"),
        P(None, None, "gz", "gx"),
        P(None, "gz", "gx"),
        P(None, "gz", "gx"),
        P("gz", "gx"),
    )
    out_specs = (
        P(None, "gz", "gx"),
        P(None, "gz", "gx"),
        P("gz", "gx"),
        P("gz", "gx"),
        P("gx"),
    )
    return jax.shard_map(
        per_device, mesh=mesh, in_specs=in_specs, out_specs=out_specs, check_vma=False
    )
```

```python
import functools
import math

import jax
import jax.numpy as jnp
import numpy as np
from jax import lax
from jax.experimental import pallas as pl
from jax.experimental.pallas import tpu as pltpu
from jax.sharding import PartitionSpec as P

DIFF = 512
FRONT_FACET = 0.3
REAR_FACET = 0.9
GAIN_SLOPE_RATE = 0.3
ALPHA_LINEWIDTH = 2.0
COUPLING = 0.5
CLOCK_DELTA = 0.3
DENSITY_LIFETIME = 2.0
GRATING_LIFE = 0.75
TRANSVERSE_DIFFUS = 0.2

MESH = pl.DeviceIdType.MESH
F32 = jnp.float32
BF16 = jnp.bfloat16

NGX = 8
NGZ = 32
ROWS = 64
COLS = 256
OWN = 8
LANES = 128
RADIX = 16
WIDTH = 2048
POWER = 16.0
SPAN = 210.0
TINY = 1e-30


def tables():
    ka = np.arange(RADIX, dtype=np.float64)
    bb = np.arange(LANES, dtype=np.float64)
    twist = 2.0 * np.pi * ka[:, None] * bb[None, :] / WIDTH
    wavenum = np.arange(RADIX)[:, None] + RADIX * np.arange(LANES)[None, :]
    signed = np.where(wavenum < WIDTH // 2, wavenum, wavenum - WIDTH).astype(np.float64)
    phase = signed * signed * (DIFF / (WIDTH / 2) ** 2)
    small = np.stack(
        [np.cos(twist), np.sin(twist), np.cos(phase) / WIDTH, np.sin(phase) / WIDTH]
    ).astype(np.float32)
    angle = 2.0 * np.pi * ((bb[:, None] * bb[None, :]) % LANES) / LANES
    c, s = np.cos(angle), np.sin(angle)
    forward = np.block([[c, -s], [s, c]])
    inverse = np.block([[c, s], [-s, c]])
    mats = []
    for m in (forward, inverse):
        high = m.astype(np.float32).astype(jnp.bfloat16)
        low = (m - high.astype(np.float64)).astype(np.float32).astype(jnp.bfloat16)
        mats += [high, low]
    return np.stack(mats), small


def encode(v, inverse_scale):
    t = jnp.log2(1.0 + jnp.abs(v) * inverse_scale) * POWER
    return jnp.exp2(jnp.where(v < 0.0, -t, t))


def decode(y, scale):
    t = jnp.log2(y.astype(F32)) * (1.0 / POWER)
    u = (jnp.exp2(jnp.abs(t)) - 1.0) * scale
    return jnp.where(t < 0.0, -u, u)


def largest(block):
    return jnp.max(jnp.max(block, axis=0, keepdims=True), axis=1, keepdims=True)


def dft(values, sign):
    n = len(values)
    if n == 1:
        return values
    even = dft(values[0::2], sign)
    odd = dft(values[1::2], sign)
    low, high = [], []
    for k in range(n // 2):
        angle = 2.0 * math.pi * k / n
        c, s = math.cos(angle), sign * math.sin(angle)
        re, im = odd[k]
        if k == 0:
            tr, ti = re, im
        elif 4 * k == n:
            tr, ti = (-im, re) if s > 0 else (im, -re)
        elif 8 * k == n:
            h = c
            tr, ti = ((re - im) * h, (re + im) * h) if s > 0 else ((re + im) * h, (im - re) * h)
        elif 8 * k == 3 * n:
            h = -c
            tr, ti = ((-re - im) * h, (re - im) * h) if s > 0 else ((im - re) * h, (-re - im) * h)
        else:
            tr, ti = re * c - im * s, re * s + im * c
        er, ei = even[k]
        low.append((er + tr, ei + ti))
        high.append((er - tr, ei - ti))
    return low + high


def split(x):
    high = x.astype(BF16)
    return high, (x - high.astype(F32)).astype(BF16)


def product(xh, xl, w, which):
    high, low = w[2 * which], w[2 * which + 1]
    a = jnp.dot(xh[...], high, preferred_element_type=F32)
    a += jnp.dot(xl[...], high, preferred_element_type=F32)
    return a + jnp.dot(xh[...], low, preferred_element_type=F32)


def diffract(uv, out, w, tb, xh, xl):
    tile = 8 * RADIX
    for field in range(2):
        points = [(uv[2 * field, a], uv[2 * field + 1, a]) for a in range(RADIX)]
        for k, (re, im) in enumerate(dft(points, -1.0)):
            c, s = tb[0, k : k + 1, :], tb[1, k : k + 1, :]
            row = pl.ds(tile * field + 8 * k, 8)
            h, l = split(re * c + im * s)
            xh[row, 0:LANES], xl[row, 0:LANES] = h, l
            h, l = split(im * c - re * s)
            xh[row, LANES:], xl[row, LANES:] = h, l
    for field in range(2):
        half = pl.ds(tile * field, tile)
        spectrum = product(xh.at[half], xl.at[half], w, 0)
        for k in range(RADIX):
            row = slice(8 * k, 8 * k + 8)
            c, s = tb[2, k : k + 1, :], tb[3, k : k + 1, :]
            re, im = spectrum[row, :LANES], spectrum[row, LANES:]
            at = pl.ds(tile * field + 8 * k, 8)
            h, l = split(re * c - im * s)
            xh[at, 0:LANES], xl[at, 0:LANES] = h, l
            h, l = split(re * s + im * c)
            xh[at, LANES:], xl[at, LANES:] = h, l
    for field in range(2):
        half = pl.ds(tile * field, tile)
        back = product(xh.at[half], xl.at[half], w, 1)
        points = []
        for k in range(RADIX):
            row = slice(8 * k, 8 * k + 8)
            c, s = tb[0, k : k + 1, :], tb[1, k : k + 1, :]
            re, im = back[row, :LANES], back[row, LANES:]
            points.append((re * c - im * s, im * c + re * s))
        for a, (re, im) in enumerate(dft(points, 1.0)):
            out[2 * field, a] = re
            out[2 * field + 1, a] = im


def revised(v, wave, level, mirror, loss, c, m, lap):
    vfr, vfi, vbr, vbi = v
    fr, fi, br, bi = wave
    e = level - 1.0
    hr = 1.0 + 0.5 * (GAIN_SLOPE_RATE * e - loss)
    hi = 0.5 * GAIN_SLOPE_RATE * ALPHA_LINEWIDTH * e
    j = COUPLING * mirror
    pd = 2.0 * CLOCK_DELTA * GAIN_SLOPE_RATE * e * c
    hd = 2.0 * CLOCK_DELTA * m
    pr = hr * vfr - hi * vfi + j * vbi - pd * fr + hd * br
    pi = hr * vfi + hi * vfr - j * vbr - pd * fi + hd * bi
    qr = hr * vbr - hi * vbi + j * vfi - pd * br + hd * fr
    qi = hr * vbi + hi * vbr - j * vfr - pd * bi + hd * fi
    light = fr * fr + fi * fi + br * br + bi * bi
    share = (
        vfr * (fr + ALPHA_LINEWIDTH * fi)
        + vfi * (fi - ALPHA_LINEWIDTH * fr)
        + vbr * (br + ALPHA_LINEWIDTH * bi)
        + vbi * (bi - ALPHA_LINEWIDTH * br)
    )
    cn = (
        c * (1.0 - CLOCK_DELTA / DENSITY_LIFETIME - CLOCK_DELTA * GAIN_SLOPE_RATE * light)
        + TRANSVERSE_DIFFUS * lap
        + 0.5 * GAIN_SLOPE_RATE * share
    )
    mn = m * (1.0 - CLOCK_DELTA / GRATING_LIFE) + COUPLING * (
        vfi * br - vfr * bi + vbi * fr - vbr * fi
    )
    return pr, pi, qr, qi, cn, mn


def place_of(g, b):
    x, zh, core = lax.div(b, 2), lax.rem(b, 2), lax.rem(g, 2)
    pos = x + zh * (7 - 2 * x)
    return pos + core * (7 - 2 * pos)


def owner_of(g, j):
    core = lax.rem(g, 2)
    pos = j + core * (7 - 2 * j)
    far = lax.div(pos, 4)
    return 2 * pos * (1 - far) + (2 * (7 - pos) + 1) * far


def rows_at(j):
    return pl.ds(pl.multiple_of(j * OWN, OWN), OWN)


def iota(axis):
    return lax.broadcasted_iota(jnp.int32, (OWN, LANES), axis)


def exchange_kernel(
    p_h, q_h, c_h, m_h, f_h, b_h, n_h, g_h, l_h, w_h, t_h,
    oc, oe, os,
    pq, w, tb, ch, co, ax, rc, ra, sg, rh, st, uv, vv, xh, xl,
    hs, hr, sacc, sb, sr, s2b, s2, s3b, s3, vo, eo,
    ls, ss, rs, cs, cr, hss, hrs, zs, zr,
):
    g, b = lax.axis_index("gz"), lax.axis_index("gx")
    me = place_of(g, b)
    started = []

    g_up, g_down = lax.rem(g + 1, NGZ), lax.rem(g + NGZ - 1, NGZ)
    chain = g * NGX + me
    after = lax.rem(chain + 1, NGZ * NGX)
    before = lax.rem(chain + NGZ * NGX - 1, NGZ * NGX)

    def row_device(q):
        qg = lax.div(q, NGX)
        return qg, owner_of(qg, lax.rem(q, NGX))

    dev_after, dev_before = row_device(after), row_device(before)
    x_peers = [(g, lax.rem(b + k, NGX)) for k in range(1, NGX)]
    z_peers = [(lax.rem(g + 2 * k, NGZ), b) for k in range(1, NGZ // 2)]
    twin = (g + 1 - 2 * lax.rem(g, 2), b)
    greet = x_peers + z_peers + [twin, (g_up, b), (g_down, b), dev_after, dev_before]
    barrier = pltpu.get_barrier_semaphore()
    for peer in greet:
        pl.semaphore_signal(barrier, inc=1, device_id=peer, device_id_type=MESH)

    loads = [
        (p_h, pq.at[0:2]),
        (q_h, pq.at[2:4]),
        (c_h, pq.at[4]),
        (m_h, pq.at[5]),
        (w_h, w),
        (t_h, tb),
        (l_h, sg.at[6]),
    ]
    for step, base in ((3, 0), (2, 7), (1, 13)):
        loads += [
            (f_h.at[step], sg.at[base : base + 2]),
            (b_h.at[step], sg.at[base + 2 : base + 4]),
            (n_h.at[step], sg.at[base + 4]),
            (g_h.at[step], sg.at[base + 5]),
        ]
    loads = [pltpu.make_async_copy(src, dst, ls.at[i]) for i, (src, dst) in enumerate(loads)]
    for load in loads[6:11] + loads[:6] + loads[11:]:
        load.start()

    pl.semaphore_wait(barrier, len(greet))

    def remote(src, dst, send, recv, device):
        copy = pltpu.make_async_remote_copy(
            src_ref=src, dst_ref=dst, send_sem=send, recv_sem=recv,
            device_id=device, device_id_type=MESH,
        )
        copy.start()
        started.append(copy)
        return copy

    edge = [
        remote(p_h.at[:, 0:8, :], ch.at[0], cs.at[0], cr.at[0], (g_down, b)),
        remote(q_h.at[:, 56:64, :], ch.at[1], cs.at[1], cr.at[1], (g_up, b)),
    ]

    def spread(ident, src_of, dst):
        got = []
        for k in range(1, NGX):
            peer = lax.rem(b + k, NGX)
            src = src_of(peer, place_of(g, peer))
            got.append(remote(src, dst, ss.at[ident, k], rs.at[ident, k], (g, peer)))
        own = pltpu.make_async_copy(src_of(b, me), dst, rs.at[ident, 0])
        own.start()
        return got, own

    def arrive(group):
        for copies, own in group:
            for copy in copies:
                copy.wait_recv()
            own.wait()

    def planes(ident, first, last):
        return [
            spread(ident, lambda _, j: sg.at[first:last, rows_at(j), :], rh.at[first:last, b])
        ]

    for load in loads[6:11]:
        load.wait()
    got_hist = {3: planes(3, 0, 7)}
    for load in loads[:4]:
        load.wait()
    top_c = largest(jnp.max(jnp.abs(pq[4]).reshape(8, 8, COLS), axis=0))
    top_m = largest(jnp.max(jnp.abs(pq[5]).reshape(8, 8, COLS), axis=0))
    top_u = jnp.max(jnp.abs(pq[0:4]).reshape(32, 8, COLS), axis=0)
    sc_c = jnp.maximum(top_c, TINY) * (1.0 / SPAN)
    sc_m = jnp.maximum(top_m, TINY) * (1.0 / SPAN)
    for i, sc in ((4, sc_c), (5, sc_m)):
        inv = 1.0 / sc
        for t in range(8):
            rows = slice(8 * t, 8 * t + 8)
            co[i, rows] = encode(pq[i, rows], inv).astype(BF16)

    got_cm = [spread(0, lambda _, j: co.at[4:6, rows_at(j), :], rc.at[4:6, b])]

    for copy in edge:
        copy.wait_recv()
    halo = jnp.maximum(jnp.max(jnp.abs(ch[0]), axis=0), jnp.max(jnp.abs(ch[1]), axis=0))
    first_block, last_block = g == 0, g == NGZ - 1
    use_halo_top = jnp.where(first_block & last_block, 0.0, 1.0)
    top_u = largest(jnp.maximum(top_u, halo * use_halo_top))
    sc_u = jnp.maximum(top_u, TINY) * (1.0 / SPAN)
    inv = 1.0 / sc_u
    wide_row = lax.broadcasted_iota(jnp.int32, (OWN, COLS), 0)
    for part in range(2):
        for t in range(8):
            rows = slice(8 * t, 8 * t + 8)
            block = pltpu.roll(pq[part, rows], 7, 0)
            if t < 7:
                edge_row = pq[part, 8 * t + 8 : 8 * t + 9]
            else:
                edge_row = jnp.where(
                    last_block, FRONT_FACET * pq[2 + part, 63:64], ch[0, part, 0:1]
                )
            block = jnp.where(wide_row == 7, edge_row, block)
            co[part, rows] = encode(block, inv).astype(BF16)
            block = pltpu.roll(pq[2 + part, rows], 1, 0)
            if t > 0:
                edge_row = pq[2 + part, 8 * t - 1 : 8 * t]
            else:
                edge_row = jnp.where(first_block, REAR_FACET * pq[part, 0:1], ch[1, part, 7:8])
            block = jnp.where(wide_row == 0, edge_row, block)
            co[2 + part, rows] = encode(block, inv).astype(BF16)
    row, lane = iota(0), iota(1)
    ax[...] = jnp.where(row == 0, sc_u, jnp.where(row == 1, sc_c, sc_m))
    got_ax = [spread(2, lambda _, j: ax, ra.at[b])]
    got_uv = [spread(1, lambda _, j: co.at[0:4, rows_at(j), :], rc.at[0:4, b])]
    for load in loads[11:15]:
        load.wait()
    got_hist[2] = planes(4, 7, 13)
    for load in loads[15:]:
        load.wait()
    got_hist[1] = planes(5, 13, 17) + planes(6, 17, 19)

    for load in loads[4:6]:
        load.wait()
    arrive(got_ax)
    arrive(got_uv)
    for a in range(RADIX):
        src, half = a // 2, pl.ds(LANES * (a % 2), LANES)
        scale = ra[src, 0:1, :]
        for i in range(4):
            uv[i, a] = decode(rc[i, src, :, half], scale)
    diffract(uv, vv, w, tb, xh, xl)

    arrive(got_cm)
    for a in range(RADIX):
        src, half = a // 2, pl.ds(LANES * (a % 2), LANES)
        for i in (4, 5):
            st[i, a] = decode(rc[i, src, :, half], ra[src, i - 3 : i - 2, :])
    weight = 1.0 + (2.0 / (ROWS * NGZ - 1)) * (row + chain * OWN).astype(F32)
    for a in range(RADIX):
        sacc[a] = weight * st[4, a]

    first_rows, last_rows = chain == 0, chain == NGZ * NGX - 1

    def lateral(a):
        c = st[4, a]
        left, right = pltpu.roll(c, 1, 1), pltpu.roll(c, LANES - 1, 1)
        left_in = pltpu.roll(st[4, a - 1], 1, 1) if a > 0 else jnp.zeros_like(c)
        right_in = (
            pltpu.roll(st[4, a + 1], LANES - 1, 1) if a < RADIX - 1 else jnp.zeros_like(c)
        )
        left = jnp.where(lane == 0, left_in, left)
        right = jnp.where(lane == LANES - 1, right_in, right)
        return c, left, right

    halos = None
    for step in (3, 2, 1):
        slot = 3 - step
        base = (0, 7, 13)[slot]
        arrive(got_hist[step])
        laps = []
        for a in range(RADIX):
            c, left, right = lateral(a)
            uv[0, a] = right - 2.0 * c + left
        for a in range(RADIX):
            src, half = a // 2, pl.ds(LANES * (a % 2), LANES)
            past = [rh[base + i, src, :, half].astype(F32) for i in range(6)]
            new = revised(
                [vv[i, a] for i in range(4)], past[:4], past[4], past[5],
                rh[6, src, :, half].astype(F32), st[4, a], st[5, a], uv[0, a],
            )
            for i in range(6):
                st[i, a] = new[i]
            sacc[a] += weight * new[4]
            for i in range(2):
                hs[slot, 0, i, :, pl.ds(LANES * a, LANES)] = new[i][0:1]
                hs[slot, 1, i, :, pl.ds(LANES * a, LANES)] = new[2 + i][7:8]
        halos = [
            remote(hs.at[slot, 0], hr.at[slot, 0], hss.at[slot, 0], hrs.at[slot, 0], dev_before),
            remote(hs.at[slot, 1], hr.at[slot, 1], hss.at[slot, 1], hrs.at[slot, 1], dev_after),
        ]
        if step == 1:
            for a in range(RADIX):
                half = pl.ds(LANES * (a % 2), LANES)
                sb[a // 2, :, half] = jnp.sum(sacc[a], axis=0, keepdims=True)
            got_s = [spread(10, lambda peer, j: sb.at[peer], sr.at[b])]
            scales = []
            for i in (4, 5):
                top = jnp.abs(st[i, 0])
                for a in range(1, RADIX):
                    top = jnp.maximum(top, jnp.abs(st[i, a]))
                sc = jnp.maximum(largest(top), TINY) * (1.0 / SPAN)
                scales.append(sc)
                inv = 1.0 / sc
                for a in range(RADIX):
                    half = pl.ds(LANES * (a % 2), LANES)
                    vo[i, a // 2, :, half] = encode(st[i, a], inv).astype(BF16)
            got_out = [spread(7, lambda peer, j: vo.at[4:6, peer], oc.at[4:6, me])]
        for copy in halos:
            copy.wait_recv()
        if step == 1:
            arrive(got_s)
            total = sr[0]
            for k in range(1, NGX):
                total = total + sr[k]
            s3b[...] = total
            s3[lax.rem(g, 2)] = total
            pair = remote(s3b, s3.at[lax.rem(g, 2)], zs.at[0], zr.at[0], twin)
        energy = [jnp.zeros((OWN, LANES), F32), jnp.zeros((OWN, LANES), F32)]
        for a in range(RADIX):
            cols = pl.ds(LANES * a, LANES)
            for i in range(2):
                edge_row = jnp.where(
                    last_rows, FRONT_FACET * st[2 + i, a, 7:8], hr[slot, 0, i, :, cols]
                )
                u = jnp.where(row == 7, edge_row, pltpu.roll(st[i, a], 7, 0))
                edge_row = jnp.where(
                    first_rows, REAR_FACET * st[i, a, 0:1], hr[slot, 1, i, :, cols]
                )
                q = jnp.where(row == 0, edge_row, pltpu.roll(st[2 + i, a], 1, 0))
                uv[i, a] = u
                uv[2 + i, a] = q
                if step == 1:
                    energy = [energy[0] + u * u, energy[1] + q * q]
        if step == 1:
            norms = [jnp.sum(e, axis=1, keepdims=True) for e in energy]
            norm = jnp.sqrt(jnp.max(jnp.maximum(norms[0], norms[1]), axis=0, keepdims=True))
            sc_v = jnp.maximum(norm, TINY) * (1.0 / SPAN)
            marks = jnp.where(row == 0, sc_v, jnp.where(row == 1, scales[0], scales[1]))
            for block in range(NGX):
                _, left, _ = lateral(2 * block)
                _, _, right = lateral(2 * block + 1)
                tile = jnp.where(lane == 0, left, marks)
                eo[block] = jnp.where(lane == LANES - 1, right, tile)
            got_out.append(spread(8, lambda peer, j: eo.at[peer], oe.at[me]))
            pair.wait_recv()
            total = s3[0] + s3[1]
            s2b[...] = total
            s2[lax.div(g, 2)] = total
            got_z = [
                remote(s2b, s2.at[lax.div(g, 2)], zs.at[k], zr.at[k], peer)
                for k, peer in enumerate(z_peers, 1)
            ]
        diffract(uv, vv, w, tb, xh, xl)

    inv = 1.0 / sc_v
    for a in range(RADIX):
        half = pl.ds(LANES * (a % 2), LANES)
        for i in range(4):
            vo[i, a // 2, :, half] = encode(vv[i, a], inv).astype(BF16)
    got_out.append(spread(9, lambda peer, j: vo.at[0:4, peer], oc.at[0:4, me]))
    for copy in got_z:
        copy.wait_recv()
    total = s2[0]
    for k in range(1, NGZ // 2):
        total = total + s2[k]
    os[...] = total * (CLOCK_DELTA / math.sqrt(ROWS * NGZ))
    arrive(got_out)
    for copy in started:
        copy.wait_send()


def final_kernel(oc, oe, os, f, bw, n, g, l, po, qo, co, mo, so, edge):
    so[...] = os[...]
    lane = lax.broadcasted_iota(jnp.int32, (OWN, COLS), 1)
    for t in range(oc.shape[1]):
        rows = pl.ds(OWN * t, OWN)
        marks = oe[t]
        scale = [marks[i : i + 1, 64:65] for i in range(3)]
        v = [decode(oc[i, t], scale[0]) for i in range(4)]
        c = decode(oc[4, t], scale[1])
        m = decode(oc[5, t], scale[2])
        left = jnp.where(lane == 0, marks[:, 0:1], pltpu.roll(c, 1, 1))
        right = jnp.where(lane == COLS - 1, marks[:, 127:128], pltpu.roll(c, COLS - 1, 1))
        wave = [x[0, i, rows].astype(F32) for x in (f, bw) for i in range(2)]
        new = revised(
            v, wave, n[0, rows].astype(F32), g[0, rows].astype(F32), l[rows].astype(F32),
            c, m, right - 2.0 * c + left,
        )
        po[0, rows], po[1, rows] = new[0], new[1]
        qo[0, rows], qo[1, rows] = new[2], new[3]
        co[rows] = new[4]
        mo[rows] = new[5]


def per_device(p, q, c, m, f, bw, n, g, l):
    mats, small = tables()
    any_space = pl.BlockSpec(memory_space=pl.ANY)
    dma = pltpu.SemaphoreType.DMA
    codes, edges, sums = pl.pallas_call(
        exchange_kernel,
        out_shape=(
            jax.ShapeDtypeStruct((6, NGX, OWN, COLS), BF16),
            jax.ShapeDtypeStruct((NGX, OWN, LANES), F32),
            jax.ShapeDtypeStruct((1, COLS), F32),
        ),
        in_specs=[any_space] * 11,
        out_specs=(any_space, any_space, pl.BlockSpec(memory_space=pltpu.VMEM)),
        scratch_shapes=[
            pltpu.VMEM((6, ROWS, COLS), F32),
            pltpu.VMEM((4, COLS, COLS), BF16),
            pltpu.VMEM((4, RADIX, LANES), F32),
            pltpu.VMEM((2, 2, OWN, COLS), F32),
            pltpu.VMEM((6, ROWS, COLS), BF16),
            pltpu.VMEM((OWN, LANES), F32),
            pltpu.VMEM((6, NGX, OWN, COLS), BF16),
            pltpu.VMEM((NGX, OWN, LANES), F32),
            pltpu.VMEM((19, ROWS, COLS), BF16),
            pltpu.VMEM((19, NGX, OWN, COLS), BF16),
            pltpu.VMEM((6, RADIX, OWN, LANES), F32),
            pltpu.VMEM((4, RADIX, OWN, LANES), F32),
            pltpu.VMEM((4, RADIX, OWN, LANES), F32),
            pltpu.VMEM((COLS, COLS), BF16),
            pltpu.VMEM((COLS, COLS), BF16),
            pltpu.VMEM((3, 2, 2, 1, WIDTH), F32),
            pltpu.VMEM((3, 2, 2, 1, WIDTH), F32),
            pltpu.VMEM((RADIX, OWN, LANES), F32),
            pltpu.VMEM((NGX, 1, COLS), F32),
            pltpu.VMEM((NGX, 1, COLS), F32),
            pltpu.VMEM((1, COLS), F32),
            pltpu.VMEM((NGZ // 2, 1, COLS), F32),
            pltpu.VMEM((1, COLS), F32),
            pltpu.VMEM((2, 1, COLS), F32),
            pltpu.VMEM((6, NGX, OWN, COLS), BF16),
            pltpu.VMEM((NGX, OWN, LANES), F32),
            dma((19,)),
            dma((11, NGX)),
            dma((11, NGX)),
            dma((2,)),
            dma((2,)),
            dma((3, 2)),
            dma((3, 2)),
            dma((NGZ // 2,)),
            dma((NGZ // 2,)),
        ],
        compiler_params=pltpu.CompilerParams(collective_id=0, has_side_effects=True),
        name="exchange",
    )(p, q, c, m, f, bw, n, g, l, jnp.asarray(mats), jnp.asarray(small))

    parts = 2
    per, rows = NGX // parts, ROWS // parts
    pair = pl.BlockSpec((2, rows, COLS), lambda i: (0, i, 0))
    single = pl.BlockSpec((rows, COLS), lambda i: (i, 0))
    line = pl.BlockSpec((1, COLS), lambda i: (0, 0))
    po, qo, co, mo, so = pl.pallas_call(
        functools.partial(final_kernel, edge=None),
        grid=(parts,),
        out_shape=(
            jax.ShapeDtypeStruct(p.shape, F32),
            jax.ShapeDtypeStruct(q.shape, F32),
            jax.ShapeDtypeStruct(c.shape, F32),
            jax.ShapeDtypeStruct(m.shape, F32),
            jax.ShapeDtypeStruct((1, COLS), F32),
        ),
        in_specs=[
            pl.BlockSpec((6, per, OWN, COLS), lambda i: (0, i, 0, 0)),
            pl.BlockSpec((per, OWN, LANES), lambda i: (i, 0, 0)),
            line,
            pl.BlockSpec((1, 2, rows, COLS), lambda i: (0, 0, i, 0)),
            pl.BlockSpec((1, 2, rows, COLS), lambda i: (0, 0, i, 0)),
            pl.BlockSpec((1, rows, COLS), lambda i: (0, i, 0)),
            pl.BlockSpec((1, rows, COLS), lambda i: (0, i, 0)),
            single,
        ],
        out_specs=(pair, pair, single, single, line),
        name="last_step",
    )(codes, edges, sums, f, bw, n, g, l)
    return po, qo, co, mo, so.reshape(COLS)


def solution(mesh):
    in_specs = (
        P(None, "gz", "gx"),
        P(None, "gz", "gx"),
        P("gz", "gx"),
        P("gz", "gx"),
        P(None, None, "gz", "gx"),
        P(None, None, "gz", "gx"),
        P(None, "gz", "gx"),
        P(None, "gz", "gx"),
        P("gz", "gx"),
    )
    out_specs = (
        P(None, "gz", "gx"),
        P(None, "gz", "gx"),
        P("gz", "gx"),
        P("gz", "gx"),
        P("gx"),
    )
    return jax.shard_map(
        per_device, mesh=mesh, in_specs=in_specs, out_specs=out_specs, check_vma=False
    )
```
